128 devices in a mesh: space: 32 (over z, x, core), chan: 4 (over y).
Axes of the slice: x: 4, y: 4, z: 4, core: 2. Of those that a mesh axis runs over, the one named last changes fastest.
Arguments:
- inputs: bfloat16 [512, 64, 2, 128], P('chan', 'space'), may hold values from -6 to 6
- weight_one: bfloat16 [512, 27, 512], P(None, None, 'chan'), may hold values from -0.0546875 to 0.0546875
- weight_two: bfloat16 [512, 27, 512], P(None, None, 'chan'), may hold values from -0.0546875 to 0.0546875
- cotangent: bfloat16 [512, 64, 2, 128], P('chan', 'space'), may hold values from -6 to 6
Outputs:
- result: bfloat16 [512, 64, 2, 128], P('chan', 'space')
- input_grad: bfloat16 [512, 64, 2, 128], P('chan', 'space')
- grad_one: float32 [512, 27, 512], P('space', None, 'chan')
- grad_two: float32 [512, 27, 512], P('space', None, 'chan')
The draws below stay inside these ranges and needn't reach their ends.
All inputs are finite; a program needn't handle non-finite values.
Results may differ from the reference program's by a relative error of at most 0.02.
Values may be sent and summed in bfloat16 or wider, within the bound.
No kernel may reach another device: no remote copies, remote signals or barrier semaphores. Data moves between devices by JAX's collectives and lax.ppermute only.
A program may use at most 192 MiB of HBM per device.

```python
import jax
import jax.numpy as jnp

CH = 512
CB = 2
CW = 128
ROWS_A = 64


def block_scale(own_key, extent, pieces, least, top_value):
    def one(axis_at, parts):
        draws = jax.random.uniform(jax.random.fold_in(jax.random.fold_in(own_key, 6), axis_at), (parts,), jnp.float32, least / len(pieces), top_value / len(pieces))
        return jnp.repeat(jnp.exp(draws), extent[axis_at] // parts).reshape((-1,) + (1,) * (len(extent) - axis_at - 1))

    factor_of = one(*pieces[0])
    for cut in pieces[1:]:
        factor_of = factor_of * one(*cut)
    return factor_of


def scatter_about(own_key, extent, deviation, bound, cuts=(), dtype=jnp.bfloat16):
    drawn = jax.random.normal(own_key, extent, jnp.float32) * deviation
    if len(cuts) > 0:
        drawn = block_scale(own_key, extent, cuts, -0.22, 0.18) * drawn
    return jnp.clip(drawn, min=-bound, max=bound).astype(dtype)


def setup_inputs(seed: int = 0) -> dict:
    arg_keys = jax.random.split(jax.random.key(seed), 5)
    inputs = scatter_about(arg_keys[0], (CH, ROWS_A, CB, CW), 1.0, 6.0, ((0, 4), (1, 32)))
    weight_one = scatter_about(arg_keys[1], (CH, 27, CH), (27 * CH) ** -0.5, 0.0546875, ((2, 4),))
    weight_two = scatter_about(arg_keys[2], (CH, 27, CH), (27 * CH) ** -0.5, 0.0546875, ((2, 4),))
    cotangent = scatter_about(arg_keys[3], (CH, ROWS_A, CB, CW), 1.0, 6.0, ((0, 4), (1, 32)))
    return dict(inputs=inputs, weight_one=weight_one, weight_two=weight_two, cotangent=cotangent)


def tap_list():
    return [(i, j, k) for i in range(3) for j in range(3) for k in range(3)]


def pad_field(field):
    return jnp.pad(field, ((0, 0), (1, 1), (1, 1), (1, 1)))


def convolve(field, weight):
    padded = pad_field(field)
    extent_a, extent_b, extent_w = field.shape[1], field.shape[2], field.shape[3]
    totals = jnp.zeros((weight.shape[2], extent_a * extent_b * extent_w), jnp.float32)
    for tap_index, (i, j, k) in enumerate(tap_list()):
        window = padded[:, i:i + extent_a, j:j + extent_b, k:k + extent_w].reshape(field.shape[0], -1)
        totals = totals + jnp.dot(weight[:, tap_index, :].T, window, preferred_element_type=jnp.float32)
    return totals.reshape(weight.shape[2], extent_a, extent_b, extent_w)


def transposed(grad_field, weight):
    padded = pad_field(grad_field)
    extent_a, extent_b, extent_w = grad_field.shape[1], grad_field.shape[2], grad_field.shape[3]
    totals = jnp.zeros((weight.shape[0], extent_a * extent_b * extent_w), jnp.float32)
    for tap_index, (i, j, k) in enumerate(tap_list()):
        window = padded[:, 2 - i:2 - i + extent_a, 2 - j:2 - j + extent_b, 2 - k:2 - k + extent_w]
        totals = totals + jnp.dot(weight[:, tap_index, :], window.reshape(grad_field.shape[0], -1), preferred_element_type=jnp.float32)
    return totals.reshape(weight.shape[0], extent_a, extent_b, extent_w)


def weight_products(field, grad_field):
    padded = pad_field(field)
    extent_a, extent_b, extent_w = field.shape[1], field.shape[2], field.shape[3]
    flat_grad = grad_field.reshape(grad_field.shape[0], -1)
    tap_rows = []
    for (i, j, k) in tap_list():
        window = padded[:, i:i + extent_a, j:j + extent_b, k:k + extent_w].reshape(field.shape[0], -1)
        tap_rows.append(jnp.dot(window, flat_grad.T, preferred_element_type=jnp.float32))
    return jnp.stack(tap_rows, axis=1)


def reference(inputs, weight_one, weight_two, cotangent):
    pre_one = convolve(inputs, weight_one)
    hidden = jax.nn.silu(pre_one).astype(jnp.bfloat16)
    result = convolve(hidden, weight_two).astype(jnp.bfloat16)
    hidden_grad = transposed(cotangent, weight_two)
    sigmoid_pre = jax.nn.sigmoid(pre_one)
    pre_grad = (hidden_grad * sigmoid_pre * (1.0 + pre_one * (1.0 - sigmoid_pre))).astype(jnp.bfloat16)
    grad_two = weight_products(hidden, cotangent)
    grad_one = weight_products(inputs, pre_grad)
    input_grad = transposed(pre_grad, weight_one).astype(jnp.bfloat16)
    return (result, input_grad, grad_one, grad_two)
```

```python
import functools

import jax
import jax.numpy as jnp
from jax import lax
from jax.experimental import pallas as pl
from jax.experimental.pallas import tpu as pltpu
from jax.sharding import PartitionSpec as P

BF16 = jnp.bfloat16
F32 = jnp.float32
TAPS = [(i, k) for i in range(3) for k in range(3)]
LANES = (slice(128, 384), slice(0, 256))


def call(kernel, out_shapes, operands, scratch=(), flops=0):
    nbytes = sum(a.size * a.dtype.itemsize for a in operands)
    nbytes += sum(a.size * a.dtype.itemsize for a in out_shapes)
    return pl.pallas_call(
        kernel,
        out_shape=tuple(out_shapes),
        in_specs=[pl.BlockSpec(memory_space=pltpu.VMEM)] * len(operands),
        out_specs=tuple(pl.BlockSpec(memory_space=pltpu.VMEM) for _ in out_shapes),
        scratch_shapes=list(scratch),
        compiler_params=pltpu.CompilerParams(vmem_limit_bytes=40 * 1024 * 1024),
        cost_estimate=pl.CostEstimate(flops=flops, bytes_accessed=nbytes, transcendentals=0),
    )(*operands)


def shape(dims, dtype):
    return jax.ShapeDtypeStruct(dims, dtype)


def row_shift(block, down):
    rows = block.shape[0]
    place = lax.broadcasted_iota(jnp.int32, block.shape, 0) % 128
    if down:
        return jnp.where(place == 0, 0.0, pltpu.roll(block, 1, 0))
    return jnp.where(place == 127, 0.0, pltpu.roll(block, rows - 1, 0))


def three_shifts(haloed):
    wide = haloed.astype(F32)
    return (row_shift(wide, False).astype(BF16), haloed, row_shift(wide, True).astype(BF16))


def conv_kernel(own, r1, r2, r3, weight, core_out, inner_out, outer_out, keep_out, send_out, field, flipped):
    y = lax.axis_index("chan")
    core = lax.axis_index("space") % 2
    for step, part in enumerate((own, r1, r2, r3)):
        place = (y ^ step) * 128
        for b in range(2):
            at = pl.multiple_of(b * 512 + place, 128)
            field[:, pl.ds(at, 128)] = part[:, b * 128 : b * 128 + 128]
    values = field[...]
    total = None
    for k in range(3):
        part = []
        for i in range(3):
            tap = 3 * i + k
            rhs = jnp.concatenate([weight[tap, :, LANES[0]], weight[tap, :, LANES[1]]], axis=0)
            part.append(jnp.dot(values, rhs, preferred_element_type=F32))
        planes = jnp.concatenate(
            [
                part[2][:128],
                part[1][:128] + part[2][128:],
                part[0][:128] + part[1][128:],
                part[0][128:],
            ],
            axis=0,
        )
        if k == 0:
            planes = row_shift(planes, True)
        elif k == 2:
            planes = row_shift(planes, False)
        total = planes if total is None else total + planes
    core_out[...] = total[128:384]
    low = total[:128].astype(BF16)
    high = total[384:].astype(BF16)
    first = core == 0
    inner_out[...] = jnp.where(first, high, low)
    outer_out[...] = jnp.where(first, low, high)
    for b in range(2):
        turned = values[:, b * 512 : b * 512 + 512].T
        for group in range(16):
            for half in range(2):
                source = group * 32 + half * 16
                flipped[half, group * 16 : group * 16 + 16, b * 256 : b * 256 + 256] = turned[
                    source : source + 16
                ]
    keep_out[...] = flipped[core]
    send_out[...] = flipped[1 - core]


def conv(own, others, weight):
    outs = [
        shape((256, 256), F32),
        shape((128, 256), BF16),
        shape((128, 256), BF16),
        shape((256, 512), BF16),
        shape((256, 512), BF16),
    ]
    scratch = [pltpu.VMEM((256, 1024), BF16), pltpu.VMEM((2, 256, 512), BF16)]
    return call(conv_kernel, outs, (own, *others, weight), scratch, flops=2 * 9 * 256 * 1024 * 256)


def conv_t_kernel(own, inner, outer, weight, o0, o1, o2, o3, haloed_out):
    y = lax.axis_index("chan")
    first = lax.axis_index("space") % 2 == 0
    low = jnp.where(first, outer[...], inner[...])
    high = jnp.where(first, inner[...], outer[...])
    haloed = jnp.concatenate([low, own[...], high], axis=0)
    haloed_out[...] = haloed
    moved = three_shifts(haloed)
    lhs = jnp.concatenate([moved[k][(2 - i) * 128 : (2 - i) * 128 + 256] for i, k in TAPS], axis=1)
    for step, out in enumerate((o0, o1, o2, o3)):
        rows = pl.ds(pl.multiple_of((y ^ step) * 128, 128), 128)
        rhs = jnp.concatenate(
            [
                jnp.concatenate([weight[3 * i + k, rows, LANES[b]] for i, k in TAPS], axis=1)
                for b in range(2)
            ],
            axis=0,
        )
        out[...] = lax.dot_general(
            lhs, rhs, (((1,), (1,)), ((), ())), preferred_element_type=F32
        ).astype(out.dtype)


def conv_t(own, inner, outer, weight):
    outs = [shape((256, 256), F32)] + [shape((256, 256), BF16)] * 3 + [shape((512, 256), BF16)]
    return call(
        conv_t_kernel, outs, (own, inner, outer, weight), flops=2 * 9 * 256 * 256 * 1024
    )


def middle_kernel(
    own, inner, outer, g0, g1, g2, g3, hidden_out, grad_out, inner_out, outer_out
):
    core = lax.axis_index("space") % 2
    first = core == 0
    zero = jnp.where(first, outer[...], inner[...]).astype(F32)
    one = jnp.where(first, inner[...], outer[...]).astype(F32)
    pre = own[...] + jnp.concatenate([zero, one], axis=0)
    hidden_grad = g0[...] + g1[...].astype(F32) + g2[...].astype(F32) + g3[...].astype(F32)
    sig = jax.nn.sigmoid(pre)
    hidden_out[...] = (pre * sig).astype(BF16)
    grad = (hidden_grad * sig * (1.0 + pre * (1.0 - sig))).astype(BF16)
    grad_out[...] = grad
    inner_out[...] = jnp.where(first, grad[128:], grad[:128])
    outer_out[...] = jnp.where(first, grad[:128], grad[128:])


def middle(own, inner, outer, parts):
    outs = [shape((256, 256), BF16)] * 2 + [shape((128, 256), BF16)] * 2
    return call(middle_kernel, outs, (own, inner, outer, *parts), flops=256 * 256 * 20)


def wprod_kernel(stage, v_own, v_far, d_own, d_far, o0, o1, o2, o3, total):
    near = three_shifts(d_own[...])
    far = three_shifts(d_far[...])
    for i, k in TAPS:
        at = (2 - i) * 128
        rhs = jnp.concatenate([near[k][at : at + 256], far[k][at : at + 256]], axis=0)
        halves = []
        for b in range(2):
            lanes = slice(b * 256, b * 256 + 256)
            lhs = jnp.concatenate([v_own[:, lanes], v_far[:, lanes]], axis=1)
            halves.append(jnp.dot(lhs, rhs, preferred_element_type=F32))
        tap = 3 * i + k
        total[tap, :, 0:128] = halves[1][:, :128]
        total[tap, :, 128:256] = halves[1][:, 128:] + halves[0][:, :128]
        total[tap, :, 256:384] = halves[0][:, 128:]
    space = lax.axis_index("space")
    if stage == "z":
        me = space // 8
        for step, out in enumerate((o0, o1, o2, o3)):
            rows = pl.ds(pl.multiple_of((me ^ step) * 64, 64), 64)
            out[...] = total[:, rows, :].astype(out.dtype)
    else:
        me = (space // 2) % 4
        for step, out in enumerate((o0, o1, o2, o3)):
            for z in range(4):
                rows = pl.ds(pl.multiple_of(z * 64 + (me ^ step) * 16, 16), 16)
                out[:, z * 16 : z * 16 + 16, :] = total[:, rows, :].astype(out.dtype)


def wprod(stage, v_own, v_far, d_own, d_far):
    outs = [shape((9, 64, 384), F32)] + [shape((9, 64, 384), BF16)] * 3
    return call(
        functools.partial(wprod_kernel, stage),
        outs,
        (v_own, v_far, d_own, d_far),
        [pltpu.VMEM((9, 256, 384), F32)],
        flops=2 * 18 * 256 * 512 * 256,
    )


def second_kernel(stage, own, r1, r2, r3, o0, o1, o2, o3, total):
    total[...] = own[...] + r1[...].astype(F32) + r2[...].astype(F32) + r3[...].astype(F32)
    space = lax.axis_index("space")
    me = (space // 2) % 4 if stage == "x" else space // 8
    for step, out in enumerate((o0, o1, o2, o3)):
        rows = pl.ds(pl.multiple_of((me ^ step) * 16, 16), 16)
        out[...] = total[:, rows, :].astype(out.dtype)


def second(stage, parts):
    outs = [shape((9, 16, 384), F32)] + [shape((9, 16, 384), BF16)] * 3
    return call(
        functools.partial(second_kernel, stage), outs, parts, [pltpu.VMEM((9, 64, 384), F32)]
    )


def last_kernel(own, r1, r2, r3, out):
    for i, k in TAPS:
        tap = 3 * i + k
        total = own[tap] + r1[tap].astype(F32) + r2[tap].astype(F32) + r3[tap].astype(F32)
        for j in range(3):
            out[:, 9 * i + 3 * j + k, :] = total[:, (2 - j) * 128 : (2 - j) * 128 + 128]


def last(parts):
    return call(last_kernel, [shape((16, 27, 128), F32)], parts)[0]


def chip(z, x, core):
    return (z * 4 + x) * 2 + core


EVERY = [(z, x, core) for z in range(4) for x in range(4) for core in range(2)]


def over_chan(step):
    return [(i, i ^ step) for i in range(4)]


def over(stage, step):
    if stage == "z":
        return [(chip(z, x, c), chip(z ^ step, x, c)) for z, x, c in EVERY]
    return [(chip(z, x, c), chip(z, x ^ step, c)) for z, x, c in EVERY]


CORES = [(i, i ^ 1) for i in range(32)]
NEIGHBOURS = [(i, i + 1 if i % 2 else i - 1) for i in range(1, 31)]


def swap_halo(inner, outer):
    return lax.ppermute(inner, "space", CORES), lax.ppermute(outer, "space", NEIGHBOURS)


def cells_major(field):
    return field.transpose(1, 3, 2, 0).reshape(256, 256)


def channels_major(block):
    return block.reshape(2, 128, 2, 128).transpose(3, 0, 2, 1).astype(BF16)


def relaid(weight):
    split = weight.reshape(512, 3, 3, 3, 128)[:, :, ::-1]
    return split.transpose(1, 3, 0, 2, 4).reshape(9, 512, 384)


def gather_chan(block):
    return [lax.ppermute(block, "chan", over_chan(step)) for step in (1, 2, 3)]


def scatter_chan(parts):
    return [parts[0]] + [
        lax.ppermute(parts[step], "chan", over_chan(step)) for step in (1, 2, 3)
    ]


def scatter_space(stage, parts):
    return [parts[0]] + [
        lax.ppermute(parts[step], "space", over(stage, step)) for step in (1, 2, 3)
    ]


def add_halo(own, inner, outer):
    first = lax.axis_index("space") % 2 == 0
    zero = jnp.where(first, outer, inner).astype(F32)
    one = jnp.where(first, inner, outer).astype(F32)
    return own + jnp.concatenate([zero, one], axis=0)


def body(inputs, weight_one, weight_two, cotangent):
    core = lax.axis_index("space") % 2
    x_own = cells_major(inputs)
    c_own = cells_major(cotangent)
    x_others = gather_chan(x_own)
    c_inner, c_outer = swap_halo(
        lax.dynamic_slice_in_dim(c_own, (1 - core) * 128, 128, 0),
        lax.dynamic_slice_in_dim(c_own, core * 128, 128, 0),
    )
    w_two = relaid(weight_two)
    w_one = relaid(weight_one)
    *hidden_parts, c_haloed = conv_t(c_own, c_inner, c_outer, w_two)
    hidden_parts = scatter_chan(hidden_parts)
    c_far = lax.ppermute(c_haloed, "space", CORES)

    pre, low, high, x_keep, x_send = conv(x_own, x_others, w_one)
    low, high = swap_halo(low, high)
    x_far = lax.ppermute(x_send, "space", CORES)
    hidden, grad, g_inner, g_outer = middle(pre, low, high, hidden_parts)

    g_inner, g_outer = swap_halo(g_inner, g_outer)
    h_others = gather_chan(hidden)
    *input_parts, g_haloed = conv_t(grad, g_inner, g_outer, w_one)
    input_parts = scatter_chan(input_parts)
    g_far = lax.ppermute(g_haloed, "space", CORES)
    one = scatter_space("x", wprod("x", x_keep, x_far, g_haloed, g_far))

    result, low, high, h_keep, h_send = conv(hidden, h_others, w_two)
    low, high = swap_halo(low, high)
    h_far = lax.ppermute(h_send, "space", CORES)
    two = scatter_space("z", wprod("z", h_keep, h_far, c_haloed, c_far))

    grad_one = last(scatter_space("z", second("z", one)))
    grad_two = last(scatter_space("x", second("x", two)))
    input_grad = sum(part.astype(F32) for part in input_parts)
    return (
        channels_major(add_halo(result, low, high)),
        channels_major(input_grad),
        grad_one,
        grad_two,
    )


def solution(mesh):
    placed = (
        P("chan", "space", None, None),
        P(None, None, "chan"),
        P(None, None, "chan"),
        P("chan", "space", None, None),
    )
    return jax.shard_map(
        body,
        mesh=mesh,
        in_specs=placed,
        out_specs=(
            P("chan", "space", None, None),
            P("chan", "space", None, None),
            P("space", None, "chan"),
            P("space", None, "chan"),
        ),
        check_vma=False,
    )
```

```python
import functools

import jax
import jax.numpy as jnp
from jax import lax
from jax.experimental import pallas as pl
from jax.experimental.pallas import tpu as pltpu
from jax.sharding import PartitionSpec as P

BF16 = jnp.bfloat16
F32 = jnp.float32
MIB = 1024 * 1024
TAPS = [(i, k) for i in range(3) for k in range(3)]
MET = ((1, 0), (2, 1))


def pair(weight, i, k, b, rows=slice(None)):
    return [weight[9 * i + 3 * j + k, rows, :] for j in MET[b]]


def call(kernel, out_shapes, operands, scratch=(), flops=0, vmem=16):
    nbytes = sum(a.size * a.dtype.itemsize for a in operands)
    nbytes += sum(a.size * a.dtype.itemsize for a in out_shapes)
    return pl.pallas_call(
        kernel,
        out_shape=tuple(out_shapes),
        in_specs=[pl.BlockSpec(memory_space=pltpu.VMEM)] * len(operands),
        out_specs=tuple(pl.BlockSpec(memory_space=pltpu.VMEM) for _ in out_shapes),
        scratch_shapes=list(scratch),
        compiler_params=pltpu.CompilerParams(vmem_limit_bytes=vmem * MIB),
        cost_estimate=pl.CostEstimate(flops=flops, bytes_accessed=nbytes, transcendentals=0),
    )(*operands)


def shape(dims, dtype):
    return jax.ShapeDtypeStruct(dims, dtype)


def row_shift(block, down):
    rows = block.shape[0]
    place = lax.broadcasted_iota(jnp.int32, block.shape, 0) % 128
    if down:
        return jnp.where(place == 0, 0.0, pltpu.roll(block, 1, 0))
    return jnp.where(place == 127, 0.0, pltpu.roll(block, rows - 1, 0))


def three_shifts(haloed):
    wide = haloed.astype(F32)
    return (row_shift(wide, False).astype(BF16), haloed, row_shift(wide, True).astype(BF16))


def conv_kernel(own, r1, r2, r3, weight, core_out, inner_out, outer_out, keep_out, send_out, field, flipped):
    y = lax.axis_index("chan")
    core = lax.axis_index("space") % 2
    for step, part in enumerate((own, r1, r2, r3)):
        place = (y ^ step) * 128
        for b in range(2):
            at = pl.multiple_of(b * 512 + place, 128)
            field[:, pl.ds(at, 128)] = part[:, b * 128 : b * 128 + 128]
    values = field[...]
    total = None
    for k in range(3):
        part = []
        for i in range(3):
            rhs = jnp.concatenate(
                [jnp.concatenate(pair(weight, i, k, b), axis=1) for b in range(2)], axis=0
            )
            part.append(jnp.dot(values, rhs, preferred_element_type=F32))
        planes = jnp.concatenate(
            [
                part[2][:128],
                part[1][:128] + part[2][128:],
                part[0][:128] + part[1][128:],
                part[0][128:],
            ],
            axis=0,
        )
        if k == 0:
            planes = row_shift(planes, True)
        elif k == 2:
            planes = row_shift(planes, False)
        total = planes if total is None else total + planes
    core_out[...] = total[128:384]
    low = total[:128].astype(BF16)
    high = total[384:].astype(BF16)
    first = core == 0
    inner_out[...] = jnp.where(first, high, low)
    outer_out[...] = jnp.where(first, low, high)
    for b in range(2):
        turned = values[:, b * 512 : b * 512 + 512].T
        for group in range(16):
            for half in range(2):
                source = group * 32 + half * 16
                flipped[half, group * 16 : group * 16 + 16, b * 256 : b * 256 + 256] = turned[
                    source : source + 16
                ]
    keep_out[...] = flipped[core]
    send_out[...] = flipped[1 - core]


def conv(own, others, weight):
    outs = [
        shape((256, 256), F32),
        shape((128, 256), BF16),
        shape((128, 256), BF16),
        shape((256, 512), BF16),
        shape((256, 512), BF16),
    ]
    scratch = [pltpu.VMEM((256, 1024), BF16), pltpu.VMEM((2, 256, 512), BF16)]
    return call(conv_kernel, outs, (own, *others, weight), scratch, flops=2 * 9 * 256 * 1024 * 256)


def conv_t_kernel(own, inner, outer, weight, o0, o1, o2, o3, haloed_out):
    y = lax.axis_index("chan")
    first = lax.axis_index("space") % 2 == 0
    low = jnp.where(first, outer[...], inner[...])
    high = jnp.where(first, inner[...], outer[...])
    haloed = jnp.concatenate([low, own[...], high], axis=0)
    haloed_out[...] = haloed
    moved = three_shifts(haloed)
    lhs = jnp.concatenate([moved[k][(2 - i) * 128 : (2 - i) * 128 + 256] for i, k in TAPS], axis=1)
    for step, out in enumerate((o0, o1, o2, o3)):
        rows = pl.ds(pl.multiple_of((y ^ step) * 128, 128), 128)
        rhs = jnp.concatenate(
            [
                jnp.concatenate(sum([pair(weight, i, k, b, rows) for i, k in TAPS], []), axis=1)
                for b in range(2)
            ],
            axis=0,
        )
        out[...] = lax.dot_general(
            lhs, rhs, (((1,), (1,)), ((), ())), preferred_element_type=F32
        ).astype(out.dtype)


def conv_t(own, inner, outer, weight):
    outs = [shape((256, 256), F32)] + [shape((256, 256), BF16)] * 3 + [shape((512, 256), BF16)]
    return call(
        conv_t_kernel, outs, (own, inner, outer, weight), flops=2 * 9 * 256 * 256 * 1024
    )


def middle_kernel(
    own, inner, outer, g0, g1, g2, g3, hidden_out, grad_out, inner_out, outer_out
):
    core = lax.axis_index("space") % 2
    first = core == 0
    zero = jnp.where(first, outer[...], inner[...]).astype(F32)
    one = jnp.where(first, inner[...], outer[...]).astype(F32)
    pre = own[...] + jnp.concatenate([zero, one], axis=0)
    hidden_grad = g0[...] + g1[...].astype(F32) + g2[...].astype(F32) + g3[...].astype(F32)
    sig = jax.nn.sigmoid(pre)
    hidden_out[...] = (pre * sig).astype(BF16)
    grad = (hidden_grad * sig * (1.0 + pre * (1.0 - sig))).astype(BF16)
    grad_out[...] = grad
    inner_out[...] = jnp.where(first, grad[128:], grad[:128])
    outer_out[...] = jnp.where(first, grad[:128], grad[128:])


def middle(own, inner, outer, parts):
    outs = [shape((256, 256), BF16)] * 2 + [shape((128, 256), BF16)] * 2
    return call(middle_kernel, outs, (own, inner, outer, *parts), flops=256 * 256 * 20, vmem=8)


def wprod_kernel(stage, v_own, v_far, d_own, d_far, o0, o1, o2, o3, total):
    near = three_shifts(d_own[...])
    far = three_shifts(d_far[...])
    for i, k in TAPS:
        at = (2 - i) * 128
        rhs = jnp.concatenate([near[k][at : at + 256], far[k][at : at + 256]], axis=0)
        halves = []
        for b in range(2):
            lanes = slice(b * 256, b * 256 + 256)
            lhs = jnp.concatenate([v_own[:, lanes], v_far[:, lanes]], axis=1)
            halves.append(jnp.dot(lhs, rhs, preferred_element_type=F32))
        tap = 3 * i + k
        total[tap, :, 0:128] = halves[1][:, :128]
        total[tap, :, 128:256] = halves[1][:, 128:] + halves[0][:, :128]
        total[tap, :, 256:384] = halves[0][:, 128:]
    space = lax.axis_index("space")
    if stage == "z":
        me = space // 8
        for step, out in enumerate((o0, o1, o2, o3)):
            rows = pl.ds(pl.multiple_of((me ^ step) * 64, 64), 64)
            out[...] = total[:, rows, :].astype(out.dtype)
    else:
        me = (space // 2) % 4
        for step, out in enumerate((o0, o1, o2, o3)):
            for z in range(4):
                rows = pl.ds(pl.multiple_of(z * 64 + (me ^ step) * 16, 16), 16)
                out[:, z * 16 : z * 16 + 16, :] = total[:, rows, :].astype(out.dtype)


def wprod(stage, v_own, v_far, d_own, d_far):
    outs = [shape((9, 64, 384), F32)] + [shape((9, 64, 384), BF16)] * 3
    return call(
        functools.partial(wprod_kernel, stage),
        outs,
        (v_own, v_far, d_own, d_far),
        [pltpu.VMEM((9, 256, 384), F32)],
        flops=2 * 18 * 256 * 512 * 256,
    )


def second_kernel(stage, own, r1, r2, r3, o0, o1, o2, o3, total):
    total[...] = own[...] + r1[...].astype(F32) + r2[...].astype(F32) + r3[...].astype(F32)
    space = lax.axis_index("space")
    me = (space // 2) % 4 if stage == "x" else space // 8
    for step, out in enumerate((o0, o1, o2, o3)):
        rows = pl.ds(pl.multiple_of((me ^ step) * 16, 16), 16)
        out[...] = total[:, rows, :].astype(out.dtype)


def second(stage, parts):
    outs = [shape((9, 16, 384), F32)] + [shape((9, 16, 384), BF16)] * 3
    return call(
        functools.partial(second_kernel, stage), outs, parts, [pltpu.VMEM((9, 64, 384), F32)], vmem=8
    )


def last_kernel(own, r1, r2, r3, out):
    for i, k in TAPS:
        tap = 3 * i + k
        total = own[tap] + r1[tap].astype(F32) + r2[tap].astype(F32) + r3[tap].astype(F32)
        for j in range(3):
            out[9 * i + 3 * j + k] = total[:, (2 - j) * 128 : (2 - j) * 128 + 128]


def last(parts):
    return call(last_kernel, [shape((27, 16, 128), F32)], parts, vmem=4)[0].transpose(1, 0, 2)


def chip(z, x, core):
    return (z * 4 + x) * 2 + core


EVERY = [(z, x, core) for z in range(4) for x in range(4) for core in range(2)]


def over_chan(step):
    return [(i, i ^ step) for i in range(4)]


def over(stage, step):
    if stage == "z":
        return [(chip(z, x, c), chip(z ^ step, x, c)) for z, x, c in EVERY]
    return [(chip(z, x, c), chip(z, x ^ step, c)) for z, x, c in EVERY]


CORES = [(i, i ^ 1) for i in range(32)]
NEIGHBOURS = [(i, i + 1 if i % 2 else i - 1) for i in range(1, 31)]


def swap_halo(inner, outer):
    return lax.ppermute(inner, "space", CORES), lax.ppermute(outer, "space", NEIGHBOURS)


def cells_major(field):
    return field.transpose(1, 3, 2, 0).reshape(256, 256)


def channels_major(block):
    return block.reshape(2, 128, 2, 128).transpose(3, 0, 2, 1).astype(BF16)


def gather_chan(block):
    return [lax.ppermute(block, "chan", over_chan(step)) for step in (1, 2, 3)]


def scatter_chan(parts):
    return [parts[0]] + [
        lax.ppermute(parts[step], "chan", over_chan(step)) for step in (1, 2, 3)
    ]


def scatter_space(stage, parts):
    return [parts[0]] + [
        lax.ppermute(parts[step], "space", over(stage, step)) for step in (1, 2, 3)
    ]


def add_halo(own, inner, outer):
    first = lax.axis_index("space") % 2 == 0
    zero = jnp.where(first, outer, inner).astype(F32)
    one = jnp.where(first, inner, outer).astype(F32)
    return own + jnp.concatenate([zero, one], axis=0)


def body(inputs, weight_one, weight_two, cotangent):
    core = lax.axis_index("space") % 2
    x_own = cells_major(inputs)
    c_own = cells_major(cotangent)
    x_others = gather_chan(x_own)
    c_inner, c_outer = swap_halo(
        lax.dynamic_slice_in_dim(c_own, (1 - core) * 128, 128, 0),
        lax.dynamic_slice_in_dim(c_own, core * 128, 128, 0),
    )
    w_two = weight_two.transpose(1, 0, 2)
    w_one = weight_one.transpose(1, 0, 2)
    *hidden_parts, c_haloed = conv_t(c_own, c_inner, c_outer, w_two)
    hidden_parts = scatter_chan(hidden_parts)
    c_far = lax.ppermute(c_haloed, "space", CORES)

    pre, low, high, x_keep, x_send = conv(x_own, x_others, w_one)
    low, high = swap_halo(low, high)
    x_far = lax.ppermute(x_send, "space", CORES)
    hidden, grad, g_inner, g_outer = middle(pre, low, high, hidden_parts)

    g_inner, g_outer = swap_halo(g_inner, g_outer)
    h_others = gather_chan(hidden)
    *input_parts, g_haloed = conv_t(grad, g_inner, g_outer, w_one)
    input_parts = scatter_chan(input_parts)
    g_far = lax.ppermute(g_haloed, "space", CORES)
    one = scatter_space("x", wprod("x", x_keep, x_far, g_haloed, g_far))

    result, low, high, h_keep, h_send = conv(hidden, h_others, w_two)
    low, high = swap_halo(low, high)
    h_far = lax.ppermute(h_send, "space", CORES)
    two = scatter_space("z", wprod("z", h_keep, h_far, c_haloed, c_far))

    grad_one = last(scatter_space("z", second("z", one)))
    grad_two = last(scatter_space("x", second("x", two)))
    input_grad = sum(part.astype(F32) for part in input_parts)
    return (
        channels_major(add_halo(result, low, high)),
        channels_major(input_grad),
        grad_one,
        grad_two,
    )


def solution(mesh):
    placed = (
        P("chan", "space", None, None),
        P(None, None, "chan"),
        P(None, None, "chan"),
        P("chan", "space", None, None),
    )
    return jax.shard_map(
        body,
        mesh=mesh,
        in_specs=placed,
        out_specs=(
            P("chan", "space", None, None),
            P("chan", "space", None, None),
            P("space", None, "chan"),
            P("space", None, "chan"),
        ),
        check_vma=False,
    )
```

```python
import functools

import jax
import jax.numpy as jnp
from jax import lax
from jax.experimental import pallas as pl
from jax.experimental.pallas import tpu as pltpu
from jax.sharding import PartitionSpec as P

BF16 = jnp.bfloat16
F32 = jnp.float32
MIB = 1024 * 1024
TAPS = [(i, k) for i in range(3) for k in range(3)]
MET = ((1, 0), (2, 1))


def pair(weight, i, k, b, rows=slice(None)):
    return [weight[9 * i + 3 * j + k, rows, :] for j in MET[b]]


def call(kernel, out_shapes, operands, scratch=(), flops=0, vmem=16):
    nbytes = sum(a.size * a.dtype.itemsize for a in operands)
    nbytes += sum(a.size * a.dtype.itemsize for a in out_shapes)
    return pl.pallas_call(
        kernel,
        out_shape=tuple(out_shapes),
        in_specs=[pl.BlockSpec(memory_space=pltpu.VMEM)] * len(operands),
        out_specs=tuple(pl.BlockSpec(memory_space=pltpu.VMEM) for _ in out_shapes),
        scratch_shapes=list(scratch),
        compiler_params=pltpu.CompilerParams(vmem_limit_bytes=vmem * MIB),
        cost_estimate=pl.CostEstimate(flops=flops, bytes_accessed=nbytes, transcendentals=0),
    )(*operands)


def shape(dims, dtype):
    return jax.ShapeDtypeStruct(dims, dtype)


def row_shift(block, down):
    rows = block.shape[0]
    place = lax.broadcasted_iota(jnp.int32, block.shape, 0) % 128
    if down:
        return jnp.where(place == 0, 0.0, pltpu.roll(block, 1, 0))
    return jnp.where(place == 127, 0.0, pltpu.roll(block, rows - 1, 0))


def three_shifts(haloed):
    wide = haloed.astype(F32)
    return (row_shift(wide, False).astype(BF16), haloed, row_shift(wide, True).astype(BF16))


def layer_call(kernel, outs, operands, weight, scratch, vmem, flops):
    vmem_spec = pl.BlockSpec(memory_space=pltpu.VMEM)
    return pl.pallas_call(
        kernel,
        out_shape=tuple(outs),
        in_specs=[vmem_spec] * (len(operands) + 1),
        out_specs=(vmem_spec,) * len(outs),
        scratch_shapes=scratch,
        compiler_params=pltpu.CompilerParams(vmem_limit_bytes=vmem * MIB),
        cost_estimate=pl.CostEstimate(flops=flops, bytes_accessed=5 * MIB, transcendentals=0),
    )(*operands, weight)


def conv_kernel(own, r1, r2, r3, three, weight, core_out, inner_out, outer_out, *rest):
    *payload, field, turned = rest
    y = lax.axis_index("chan")
    space = lax.axis_index("space")
    first = space % 2 == 0
    z = space // 8
    for step, part in enumerate((own, r1, r2, r3)):
        place = y ^ step
        for b in range(2):
            at = pl.multiple_of(b * 512 + place * 128, 128)
            field[:, pl.ds(at, 128)] = part[:, b * 128 : b * 128 + 128]
        turn(part[...], turned.at[place])
    for step in range(4):
        if len(payload) == 1:
            out, at = payload[0].at[step], step
        else:
            out, at = payload[step], z ^ step
        out[:256, :] = turned[at]
        out[256:, :] = three[...]
    values = field[...]
    sums = None
    for k in range(3):
        part = []
        for i in range(3):
            rhs = jnp.concatenate(
                [jnp.concatenate(pair(weight, i, k, b), axis=1) for b in range(2)], axis=0
            )
            part.append(jnp.dot(values, rhs, preferred_element_type=F32))
        planes = jnp.concatenate(
            [
                part[2][:128],
                part[1][:128] + part[2][128:],
                part[0][:128] + part[1][128:],
                part[0][128:],
            ],
            axis=0,
        )
        if k != 1:
            planes = row_shift(planes, k == 0)
        sums = planes if sums is None else sums + planes
    core_out[...] = sums[128:384]
    low = sums[:128].astype(BF16)
    high = sums[384:].astype(BF16)
    inner_out[...] = jnp.where(first, high, low)
    outer_out[...] = jnp.where(first, low, high)


def conv(own, others, weight, three, whole):
    outs = [shape((256, 256), F32), shape((128, 256), BF16), shape((128, 256), BF16)]
    outs += [shape((4, 640, 256), BF16)] if whole else [shape((640, 256), BF16)] * 4
    scratch = [
        pltpu.VMEM((256, 1024), BF16),
        pltpu.VMEM((4, 256, 256), BF16),
    ]
    core_out, inner, outer, *payload = layer_call(
        conv_kernel, outs, (own, *others, three), weight, scratch, 16, 2 * 9 * 256 * 1024 * 256
    )
    return core_out, inner, outer, payload


def conv_t_kernel(own, inner, outer, weight, *rest):
    *outs, three_out = rest
    y = lax.axis_index("chan")
    first = lax.axis_index("space") % 2 == 0
    low = jnp.where(first, outer[...], inner[...])
    high = jnp.where(first, inner[...], outer[...])
    haloed = jnp.concatenate([low, own[...], high], axis=0)
    three_out[...] = jnp.where(first, haloed[:384], haloed[128:])
    moved = three_shifts(haloed)
    lhs = jnp.concatenate([moved[k][(2 - i) * 128 : (2 - i) * 128 + 256] for i, k in TAPS], axis=1)
    for step in range(4):
        group = step if len(outs) == 1 else y ^ step
        out = outs[0].at[step] if len(outs) == 1 else outs[step]
        rows = pl.ds(group * 128 if len(outs) == 1 else pl.multiple_of(group * 128, 128), 128)
        rhs = jnp.concatenate(
            [
                jnp.concatenate(sum([pair(weight, i, k, b, rows) for i, k in TAPS], []), axis=1)
                for b in range(2)
            ],
            axis=0,
        )
        out[...] = lax.dot_general(
            lhs, rhs, (((1,), (1,)), ((), ())), preferred_element_type=F32
        ).astype(out.dtype)


def conv_t(own, inner, outer, weight, whole):
    if whole:
        outs = [shape((4, 256, 256), BF16)]
    else:
        outs = [shape((256, 256), F32)] + [shape((256, 256), BF16)] * 3
    outs += [shape((384, 256), BF16)]
    *parts, three = layer_call(
        conv_t_kernel, outs, (own, inner, outer), weight, [], 16, 2 * 9 * 256 * 256 * 1024
    )
    return parts, three


def turn(block, out):
    turned = block.T
    for half in range(2):
        for b in range(2):
            for x in range(4):
                source = b * 128 + x * 32 + half * 16
                target = half * 128 + b * 64 + x * 16
                out[target : target + 16, :] = turned[source : source + 16]


def middle_kernel(
    own, inner, outer, g0, g1, g2, g3, hidden_out, grad_out, inner_out, outer_out
):
    first = lax.axis_index("space") % 2 == 0
    zero = jnp.where(first, outer[...], inner[...]).astype(F32)
    one = jnp.where(first, inner[...], outer[...]).astype(F32)
    pre = own[...] + jnp.concatenate([zero, one], axis=0)
    hidden_grad = g0[...] + g1[...].astype(F32) + g2[...].astype(F32) + g3[...].astype(F32)
    sig = jax.nn.sigmoid(pre)
    hidden_out[...] = (pre * sig).astype(BF16)
    grad = (hidden_grad * sig * (1.0 + pre * (1.0 - sig))).astype(BF16)
    grad_out[...] = grad
    inner_out[...] = jnp.where(first, grad[128:], grad[:128])
    outer_out[...] = jnp.where(first, grad[:128], grad[128:])


def middle(own, inner, outer, parts):
    outs = [shape((256, 256), BF16)] * 2 + [shape((128, 256), BF16)] * 2
    return call(middle_kernel, outs, (own, inner, outer, *parts), flops=256 * 256 * 20, vmem=8)


def keep_product(total, tap, product):
    total[tap, :, 0:128] = product[64:, :128]
    total[tap, :, 128:256] = product[64:, 128:] + product[:64, :128]
    total[tap, :, 256:384] = product[:64, 128:]


def wprod_kernel(late_v, v, v_far, d, d_far, o0, o1, o2, o3, d_all, v_all, sums, total, sems):
    space = lax.axis_index("space")
    core, z = space % 2, space // 8
    rows = pl.ds(pl.multiple_of(core * 128, 128), 128)
    started = []
    for step in range(4):
        v_from, d_from = (step, z ^ step) if late_v else (z ^ step, step)
        pieces = []
        for far, (v_slots, d_slots) in enumerate(((v, d), (v_far, d_far))):
            pieces += [
                (v_slots.at[v_from, rows], v_all.at[step, core ^ far]),
                (d_slots.at[d_from, pl.ds(256, 384)], d_all.at[step, core ^ far]),
            ]
        started.append(
            [
                pltpu.make_async_copy(source, target, sems.at[4 * step + at])
                for at, (source, target) in enumerate(pieces)
            ]
        )
    for copies in started:
        for copy in copies:
            copy.start()
    for step, copies in enumerate(started):
        for copy in copies:
            copy.wait()
        lhs = jnp.concatenate([v_all[step, 0], v_all[step, 1]], axis=1)
        moved = three_shifts(d_all[step].reshape(768, 256))
        for i, k in TAPS:
            at = (2 - i) * 128
            product = jnp.dot(lhs, moved[k][at : at + 512], preferred_element_type=F32)
            if step == 0:
                sums[3 * i + k] = product
            else:
                sums[3 * i + k] += product
    for tap in range(9):
        total[tap, :, 0:128] = sums[tap, 64:, :128]
        total[tap, :, 128:256] = sums[tap, 64:, 128:] + sums[tap, :64, :128]
        total[tap, :, 256:384] = sums[tap, :64, 128:]
    x = (space // 2) % 4
    for step, out in enumerate((o0, o1, o2, o3)):
        chosen = pl.ds(pl.multiple_of((x ^ step) * 16, 16), 16)
        out[...] = total[:, chosen, :].astype(out.dtype)


def wprod(late_v, v_slots, d_slots):
    hbm_spec = pl.BlockSpec(memory_space=pltpu.HBM)
    vmem_spec = pl.BlockSpec(memory_space=pltpu.VMEM)
    return pl.pallas_call(
        functools.partial(wprod_kernel, late_v),
        out_shape=(shape((9, 16, 384), F32),) + (shape((9, 16, 384), BF16),) * 3,
        in_specs=[hbm_spec] * 4,
        out_specs=(vmem_spec,) * 4,
        scratch_shapes=[
            pltpu.VMEM((4, 2, 384, 256), BF16),
            pltpu.VMEM((4, 2, 128, 256), BF16),
            pltpu.VMEM((9, 128, 256), F32),
            pltpu.VMEM((9, 64, 384), F32),
            pltpu.SemaphoreType.DMA((16,)),
        ],
        compiler_params=pltpu.CompilerParams(vmem_limit_bytes=24 * MIB),
        cost_estimate=pl.CostEstimate(
            flops=2 * 9 * 128 * 2048 * 256, bytes_accessed=4 * MIB, transcendentals=0
        ),
    )(*v_slots, *d_slots)


def last_kernel(own, r1, r2, r3, out):
    for i, k in TAPS:
        tap = 3 * i + k
        total = own[tap] + r1[tap].astype(F32) + r2[tap].astype(F32) + r3[tap].astype(F32)
        for j in range(3):
            out[9 * i + 3 * j + k] = total[:, (2 - j) * 128 : (2 - j) * 128 + 128]


def last(parts):
    return call(last_kernel, [shape((27, 16, 128), F32)], parts, vmem=4)[0].transpose(1, 0, 2)


def chip(z, x, core):
    return (z * 4 + x) * 2 + core


EVERY = [(z, x, core) for z in range(4) for x in range(4) for core in range(2)]


def over_chan(step):
    return [(i, i ^ step) for i in range(4)]


def over_z(step):
    return [(chip(z, x, c), chip(z ^ step, x, c)) for z, x, c in EVERY]


def over_x(step):
    return [(chip(z, x, c), chip(z, x ^ step, c)) for z, x, c in EVERY]


CORES = [(i, i ^ 1) for i in range(32)]
NEIGHBOURS = [(i, i + 1 if i % 2 else i - 1) for i in range(1, 31)]


def swap_halo(inner, outer):
    return lax.ppermute(inner, "space", CORES), lax.ppermute(outer, "space", NEIGHBOURS)


def cells_major(field):
    return field.transpose(1, 3, 2, 0).reshape(256, 256)


def channels_major(block):
    return block.reshape(2, 128, 2, 128).transpose(3, 0, 2, 1).astype(BF16)


def gather_chan(block):
    return [lax.ppermute(block, "chan", over_chan(step)) for step in (1, 2, 3)]


def scatter_chan(parts):
    return [parts[0]] + [
        lax.ppermute(parts[step], "chan", over_chan(step)) for step in (1, 2, 3)
    ]


def scatter_x(parts):
    return [parts[0]] + [lax.ppermute(parts[step], "space", over_x(step)) for step in (1, 2, 3)]


ALONG_Z = [[chip(z, x, c) for z in range(4)] for x in range(4) for c in range(2)]


def exchange_z(parts):
    return [parts[0]] + [lax.ppermute(parts[step], "space", over_z(step)) for step in (1, 2, 3)]


def with_far(near):
    return [near, lax.ppermute(near, "space", CORES)]


def add_halo(own, inner, outer):
    first = lax.axis_index("space") % 2 == 0
    zero = jnp.where(first, outer, inner).astype(F32)
    one = jnp.where(first, inner, outer).astype(F32)
    return own + jnp.concatenate([zero, one], axis=0)


def body(inputs, weight_one, weight_two, cotangent):
    core = lax.axis_index("space") % 2
    c_own = cells_major(cotangent)
    x_own = cells_major(inputs)
    w_two = weight_two.transpose(1, 0, 2)
    w_one = weight_one.transpose(1, 0, 2)
    c_inner, c_outer = swap_halo(
        lax.dynamic_slice_in_dim(c_own, (1 - core) * 128, 128, 0),
        lax.dynamic_slice_in_dim(c_own, core * 128, 128, 0),
    )
    x_others = gather_chan(x_own)
    hidden_parts, c_three = conv_t(c_own, c_inner, c_outer, w_two, False)
    hidden_parts = scatter_chan(hidden_parts)
    pre, low, high, payload = conv(x_own, x_others, w_one, c_three, True)
    low, high = swap_halo(low, high)
    payload, hidden_parts, low = lax.optimization_barrier((payload, hidden_parts, low))
    early = lax.all_to_all(payload[0], "space", 0, 0, tiled=True, axis_index_groups=ALONG_Z)
    hidden, grad, g_inner, g_outer = middle(pre, low, high, hidden_parts)

    h_others = gather_chan(hidden)
    g_inner, g_outer = swap_halo(g_inner, g_outer)
    h_others, g_inner, early = lax.optimization_barrier((h_others, g_inner, early))
    early = with_far(early)
    input_parts, g_three = conv_t(grad, g_inner, g_outer, w_one, True)
    result, low, high, payload = conv(hidden, h_others, w_two, g_three, False)
    late = jnp.stack(exchange_z(payload))
    low, high = swap_halo(low, high)
    input_parts, low = lax.optimization_barrier((input_parts, low))
    input_parts = lax.all_to_all(input_parts[0], "chan", 0, 0, tiled=True)
    late, input_parts, low, high = lax.optimization_barrier((late, input_parts, low, high))
    late = with_far(late)
    grad_one = last(scatter_x(wprod(False, early, late)))
    grad_two = last(scatter_x(wprod(True, late, early)))
    input_grad = jnp.sum(input_parts.astype(F32), axis=0)
    return (
        channels_major(add_halo(result, low, high)),
        channels_major(input_grad),
        grad_one,
        grad_two,
    )


def solution(mesh):
    placed = (
        P("chan", "space", None, None),
        P(None, None, "chan"),
        P(None, None, "chan"),
        P("chan", "space", None, None),
    )
    return jax.shard_map(
        body,
        mesh=mesh,
        in_specs=placed,
        out_specs=(
            P("chan", "space", None, None),
            P("chan", "space", None, None),
            P("space", None, "chan"),
            P("space", None, "chan"),
        ),
        check_vma=False,
    )
```

```python
import functools

import jax
import jax.numpy as jnp
from jax import lax
from jax.experimental import pallas as pl
from jax.experimental.pallas import tpu as pltpu
from jax.sharding import PartitionSpec as P

BF16 = jnp.bfloat16
F32 = jnp.float32
MIB = 1024 * 1024
TAPS = [(i, k) for i in range(3) for k in range(3)]
MET = ((1, 0), (2, 1))


def pair(weight, i, k, b, rows=slice(None)):
    return [weight[9 * i + 3 * j + k, rows, :] for j in MET[b]]


def call(kernel, out_shapes, operands, scratch=(), flops=0, vmem=16):
    nbytes = sum(a.size * a.dtype.itemsize for a in operands)
    nbytes += sum(a.size * a.dtype.itemsize for a in out_shapes)
    return pl.pallas_call(
        kernel,
        out_shape=tuple(out_shapes),
        in_specs=[pl.BlockSpec(memory_space=pltpu.VMEM)] * len(operands),
        out_specs=tuple(pl.BlockSpec(memory_space=pltpu.VMEM) for _ in out_shapes),
        scratch_shapes=list(scratch),
        compiler_params=pltpu.CompilerParams(vmem_limit_bytes=vmem * MIB),
        cost_estimate=pl.CostEstimate(flops=flops, bytes_accessed=nbytes, transcendentals=0),
    )(*operands)


def shape(dims, dtype):
    return jax.ShapeDtypeStruct(dims, dtype)


def row_shift(block, down):
    rows = block.shape[0]
    place = lax.broadcasted_iota(jnp.int32, block.shape, 0) % 128
    if down:
        return jnp.where(place == 0, 0.0, pltpu.roll(block, 1, 0))
    return jnp.where(place == 127, 0.0, pltpu.roll(block, rows - 1, 0))


def three_shifts(haloed):
    wide = haloed.astype(F32)
    return (row_shift(wide, False).astype(BF16), haloed, row_shift(wide, True).astype(BF16))


def layer_call(kernel, outs, operands, weight, scratch, vmem, flops):
    vmem_spec = pl.BlockSpec(memory_space=pltpu.VMEM)
    return pl.pallas_call(
        kernel,
        out_shape=tuple(outs),
        in_specs=[vmem_spec] * (len(operands) + 1),
        out_specs=(vmem_spec,) * len(outs),
        scratch_shapes=scratch,
        compiler_params=pltpu.CompilerParams(vmem_limit_bytes=vmem * MIB),
        cost_estimate=pl.CostEstimate(flops=flops, bytes_accessed=5 * MIB, transcendentals=0),
    )(*operands, weight)


def pack_kernel(own, r1, r2, r3, grad, outer, *rest):
    *payload, turned = rest
    y = lax.axis_index("chan")
    space = lax.axis_index("space")
    first, z = space % 2 == 0, space // 8
    mine, far = grad[...], outer[...]
    three = jnp.where(
        first, jnp.concatenate([far, mine], axis=0), jnp.concatenate([mine, far], axis=0)
    )
    for step, part in enumerate((own, r1, r2, r3)):
        turn(part[...], turned.at[y ^ step])
    for step, out in enumerate(payload):
        out[:256, :] = turned[z ^ step]
        out[256:, :] = three


def pack(own, others, grad, outer):
    return call(
        pack_kernel,
        [shape((640, 256), BF16)] * 4,
        (own, *others, grad, outer),
        [pltpu.VMEM((4, 256, 256), BF16)],
        flops=10**9,
        vmem=8,
    )


def conv_kernel(own, r1, r2, r3, *rest):
    y = lax.axis_index("chan")
    first = lax.axis_index("space") % 2 == 0
    if len(rest) == 5:
        weight, core_out, inner_out, outer_out, field = rest
    else:
        three, weight, core_out, inner_out, outer_out, payload, field, turned = rest
        for step, part in enumerate((own, r1, r2, r3)):
            turn(part[...], turned.at[y ^ step])
        for z in range(4):
            payload[z, :256, :] = turned[z]
            payload[z, 256:, :] = three[...]
    for step, part in enumerate((own, r1, r2, r3)):
        for b in range(2):
            at = pl.multiple_of(b * 512 + (y ^ step) * 128, 128)
            field[:, pl.ds(at, 128)] = part[:, b * 128 : b * 128 + 128]
    values = field[...]
    sums = None
    for k in range(3):
        part = []
        for i in range(3):
            rhs = jnp.concatenate(
                [jnp.concatenate(pair(weight, i, k, b), axis=1) for b in range(2)], axis=0
            )
            part.append(jnp.dot(values, rhs, preferred_element_type=F32))
        planes = jnp.concatenate(
            [
                part[2][:128],
                part[1][:128] + part[2][128:],
                part[0][:128] + part[1][128:],
                part[0][128:],
            ],
            axis=0,
        )
        if k != 1:
            planes = row_shift(planes, k == 0)
        sums = planes if sums is None else sums + planes
    core_out[...] = sums[128:384]
    low = sums[:128].astype(BF16)
    high = sums[384:].astype(BF16)
    inner_out[...] = jnp.where(first, high, low)
    outer_out[...] = jnp.where(first, low, high)


def conv(own, others, weight, three=()):
    outs = [shape((256, 256), F32), shape((128, 256), BF16), shape((128, 256), BF16)]
    outs += [shape((4, 640, 256), BF16)] * len(three)
    scratch = [pltpu.VMEM((256, 1024), BF16)]
    scratch += [pltpu.VMEM((4, 256, 256), BF16)] * len(three)
    return layer_call(
        conv_kernel, outs, (own, *others, *three), weight, scratch, 16, 2 * 9 * 256 * 1024 * 256
    )


def conv_t_kernel(own, inner, outer, weight, *rest):
    *outs, three_out = rest
    y = lax.axis_index("chan")
    first = lax.axis_index("space") % 2 == 0
    low = jnp.where(first, outer[...], inner[...])
    high = jnp.where(first, inner[...], outer[...])
    haloed = jnp.concatenate([low, own[...], high], axis=0)
    three_out[...] = jnp.where(first, haloed[:384], haloed[128:])
    moved = three_shifts(haloed)
    lhs = jnp.concatenate([moved[k][(2 - i) * 128 : (2 - i) * 128 + 256] for i, k in TAPS], axis=1)
    for step in range(4):
        group = step if len(outs) == 1 else y ^ step
        out = outs[0].at[step] if len(outs) == 1 else outs[step]
        rows = pl.ds(group * 128 if len(outs) == 1 else pl.multiple_of(group * 128, 128), 128)
        rhs = jnp.concatenate(
            [
                jnp.concatenate(sum([pair(weight, i, k, b, rows) for i, k in TAPS], []), axis=1)
                for b in range(2)
            ],
            axis=0,
        )
        out[...] = lax.dot_general(
            lhs, rhs, (((1,), (1,)), ((), ())), preferred_element_type=F32
        ).astype(out.dtype)


def conv_t(own, inner, outer, weight, whole):
    if whole:
        outs = [shape((4, 256, 256), BF16)]
    else:
        outs = [shape((256, 256), F32)] + [shape((256, 256), BF16)] * 3
    outs += [shape((384, 256), BF16)]
    *parts, three = layer_call(
        conv_t_kernel, outs, (own, inner, outer), weight, [], 16, 2 * 9 * 256 * 256 * 1024
    )
    return parts, three


def turn(block, out):
    turned = block.T
    for half in range(2):
        for b in range(2):
            for x in range(4):
                source = b * 128 + x * 32 + half * 16
                target = half * 128 + b * 64 + x * 16
                out[target : target + 16, :] = turned[source : source + 16]


def middle_kernel(
    own, inner, outer, g0, g1, g2, g3, hidden_out, grad_out, inner_out, outer_out
):
    first = lax.axis_index("space") % 2 == 0
    zero = jnp.where(first, outer[...], inner[...]).astype(F32)
    one = jnp.where(first, inner[...], outer[...]).astype(F32)
    pre = own[...] + jnp.concatenate([zero, one], axis=0)
    hidden_grad = g0[...] + g1[...].astype(F32) + g2[...].astype(F32) + g3[...].astype(F32)
    sig = jax.nn.sigmoid(pre)
    hidden_out[...] = (pre * sig).astype(BF16)
    grad = (hidden_grad * sig * (1.0 + pre * (1.0 - sig))).astype(BF16)
    grad_out[...] = grad
    inner_out[...] = jnp.where(first, grad[128:], grad[:128])
    outer_out[...] = jnp.where(first, grad[:128], grad[128:])


def middle(own, inner, outer, parts):
    outs = [shape((256, 256), BF16)] * 2 + [shape((128, 256), BF16)] * 2
    return call(middle_kernel, outs, (own, inner, outer, *parts), flops=256 * 256 * 20, vmem=8)


def keep_product(total, tap, product):
    total[tap, :, 0:128] = product[64:, :128]
    total[tap, :, 128:256] = product[64:, 128:] + product[:64, :128]
    total[tap, :, 256:384] = product[:64, 128:]


def wprod_kernel(early, early_far, late, late_far, o0, o1, o2, o3, d_all, v_all, sums, total, sems):
    space = lax.axis_index("space")
    core, z = space % 2, space // 8
    rows = pl.ds(pl.multiple_of(core * 128, 128), 128)
    planes = pl.ds(256, 384)
    started = []
    for step in range(4):
        pieces = []
        for far in range(2):
            soon = (early, early_far)[far].at[z ^ step]
            last = (late, late_far)[far].at[step]
            for layer, (v, d) in enumerate(((soon, last), (last, soon))):
                pieces += [
                    (v.at[rows], v_all.at[layer, step, core ^ far]),
                    (d.at[planes], d_all.at[layer, step, core ^ far]),
                ]
        started.append(
            [
                pltpu.make_async_copy(source, target, sems.at[8 * step + at])
                for at, (source, target) in enumerate(pieces)
            ]
        )
    for copies in started:
        for copy in copies:
            copy.start()
    for step, copies in enumerate(started):
        for copy in copies:
            copy.wait()
        for layer in range(2):
            lhs = jnp.concatenate([v_all[layer, step, 0], v_all[layer, step, 1]], axis=1)
            moved = three_shifts(d_all[layer, step].reshape(768, 256))
            for i, k in TAPS:
                at = (2 - i) * 128
                tap = 9 * layer + 3 * i + k
                product = jnp.dot(lhs, moved[k][at : at + 512], preferred_element_type=F32)
                if step == 0:
                    sums[tap] = product
                else:
                    sums[tap] += product
    for tap in range(18):
        total[tap, :, 0:128] = sums[tap, 64:, :128]
        total[tap, :, 128:256] = sums[tap, 64:, 128:] + sums[tap, :64, :128]
        total[tap, :, 256:384] = sums[tap, :64, 128:]
    x = (space // 2) % 4
    for step, out in enumerate((o0, o1, o2, o3)):
        chosen = pl.ds(pl.multiple_of((x ^ step) * 16, 16), 16)
        out[...] = total[:, chosen, :].astype(out.dtype)


def wprod(early, late):
    hbm_spec = pl.BlockSpec(memory_space=pltpu.HBM)
    vmem_spec = pl.BlockSpec(memory_space=pltpu.VMEM)
    return pl.pallas_call(
        wprod_kernel,
        out_shape=(shape((18, 16, 384), F32),) + (shape((18, 16, 384), BF16),) * 3,
        in_specs=[hbm_spec] * 4,
        out_specs=(vmem_spec,) * 4,
        scratch_shapes=[
            pltpu.VMEM((2, 4, 2, 384, 256), BF16),
            pltpu.VMEM((2, 4, 2, 128, 256), BF16),
            pltpu.VMEM((18, 128, 256), F32),
            pltpu.VMEM((18, 64, 384), F32),
            pltpu.SemaphoreType.DMA((32,)),
        ],
        compiler_params=pltpu.CompilerParams(vmem_limit_bytes=24 * MIB),
        cost_estimate=pl.CostEstimate(
            flops=4 * 9 * 128 * 2048 * 256, bytes_accessed=8 * MIB, transcendentals=0
        ),
    )(*early, *late)


def last_kernel(own, r1, r2, r3, one_out, two_out):
    for layer, out in enumerate((one_out, two_out)):
        for i, k in TAPS:
            tap = 9 * layer + 3 * i + k
            total = own[tap] + r1[tap].astype(F32) + r2[tap].astype(F32) + r3[tap].astype(F32)
            for j in range(3):
                out[9 * i + 3 * j + k] = total[:, (2 - j) * 128 : (2 - j) * 128 + 128]


def last(parts):
    outs = call(last_kernel, [shape((27, 16, 128), F32)] * 2, parts, vmem=4)
    return [out.transpose(1, 0, 2) for out in outs]


def chip(z, x, core):
    return (z * 4 + x) * 2 + core


EVERY = [(z, x, core) for z in range(4) for x in range(4) for core in range(2)]


def over_chan(step):
    return [(i, i ^ step) for i in range(4)]


def over_z(step):
    return [(chip(z, x, c), chip(z ^ step, x, c)) for z, x, c in EVERY]


def over_x(step):
    return [(chip(z, x, c), chip(z, x ^ step, c)) for z, x, c in EVERY]


CORES = [(i, i ^ 1) for i in range(32)]
NEIGHBOURS = [(i, i + 1 if i % 2 else i - 1) for i in range(1, 31)]


def swap_halo(inner, outer):
    return lax.ppermute(inner, "space", CORES), lax.ppermute(outer, "space", NEIGHBOURS)


def cells_major(field):
    return field.transpose(1, 3, 2, 0).reshape(256, 256)


def channels_major(block):
    return block.reshape(2, 128, 2, 128).transpose(3, 0, 2, 1).astype(BF16)


def gather_chan(block):
    return [lax.ppermute(block, "chan", over_chan(step)) for step in (1, 2, 3)]


def scatter_chan(parts):
    return [parts[0]] + [
        lax.ppermute(parts[step], "chan", over_chan(step)) for step in (1, 2, 3)
    ]


def scatter_x(parts):
    return [parts[0]] + [lax.ppermute(parts[step], "space", over_x(step)) for step in (1, 2, 3)]


ALONG_Z = [[chip(z, x, c) for z in range(4)] for x in range(4) for c in range(2)]


def exchange_z(parts):
    return [parts[0]] + [lax.ppermute(parts[step], "space", over_z(step)) for step in (1, 2, 3)]


def with_far(near):
    return [near, lax.ppermute(near, "space", CORES)]


def add_halo(own, inner, outer):
    first = lax.axis_index("space") % 2 == 0
    zero = jnp.where(first, outer, inner).astype(F32)
    one = jnp.where(first, inner, outer).astype(F32)
    return own + jnp.concatenate([zero, one], axis=0)


def body(inputs, weight_one, weight_two, cotangent):
    core = lax.axis_index("space") % 2
    c_own = cells_major(cotangent)
    x_own = cells_major(inputs)
    w_two = weight_two.transpose(1, 0, 2)
    w_one = weight_one.transpose(1, 0, 2)
    c_inner, c_outer = swap_halo(
        lax.dynamic_slice_in_dim(c_own, (1 - core) * 128, 128, 0),
        lax.dynamic_slice_in_dim(c_own, core * 128, 128, 0),
    )
    x_others = gather_chan(x_own)
    hidden_parts, c_three = conv_t(c_own, c_inner, c_outer, w_two, False)
    hidden_parts = scatter_chan(hidden_parts)
    pre, low, high, payload = conv(x_own, x_others, w_one, [c_three])
    low, high = swap_halo(low, high)
    payload, hidden_parts, low = lax.optimization_barrier((payload, hidden_parts, low))
    early = lax.all_to_all(payload, "space", 0, 0, tiled=True, axis_index_groups=ALONG_Z)
    hidden, grad, g_inner, g_outer = middle(pre, low, high, hidden_parts)

    h_others = gather_chan(hidden)
    g_inner, g_outer = swap_halo(g_inner, g_outer)
    h_others, g_inner, early = lax.optimization_barrier((h_others, g_inner, early))
    early = with_far(early)
    payload = pack(hidden, h_others, grad, g_outer)
    payload, grad, hidden = lax.optimization_barrier((payload, grad, hidden))
    late = exchange_z(payload)
    input_parts, _ = conv_t(grad, g_inner, g_outer, w_one, False)
    input_parts = scatter_chan(input_parts)
    result, low, high = conv(hidden, h_others, w_two)
    late, input_parts, low = lax.optimization_barrier((late, input_parts, low))
    late = with_far(jnp.stack(late))
    shares = wprod(early, late)
    shares = scatter_x(shares)
    shares[1], low, high = lax.optimization_barrier((shares[1], low, high))
    grad_one, grad_two = last(shares)
    low, high = swap_halo(low, high)
    input_grad = sum(part.astype(F32) for part in input_parts)
    return (
        channels_major(add_halo(result, low, high)),
        channels_major(input_grad),
        grad_one,
        grad_two,
    )


def solution(mesh):
    placed = (
        P("chan", "space", None, None),
        P(None, None, "chan"),
        P(None, None, "chan"),
        P("chan", "space", None, None),
    )
    return jax.shard_map(
        body,
        mesh=mesh,
        in_specs=placed,
        out_specs=(
            P("chan", "space", None, None),
            P("chan", "space", None, None),
            P("space", None, "chan"),
            P("space", None, "chan"),
        ),
        check_vma=False,
    )
```

```python
import functools

import jax
import jax.numpy as jnp
from jax import lax
from jax.experimental import pallas as pl
from jax.experimental.pallas import tpu as pltpu
from jax.sharding import PartitionSpec as P

BF16 = jnp.bfloat16
F32 = jnp.float32
MIB = 1024 * 1024
TAPS = [(i, k) for i in range(3) for k in range(3)]
MET = ((1, 0), (2, 1))


def pair(weight, i, k, b, rows=slice(None)):
    return [weight[9 * i + 3 * j + k, rows, :] for j in MET[b]]


def call(kernel, out_shapes, operands, scratch=(), flops=0, vmem=16):
    nbytes = sum(a.size * a.dtype.itemsize for a in operands)
    nbytes += sum(a.size * a.dtype.itemsize for a in out_shapes)
    return pl.pallas_call(
        kernel,
        out_shape=tuple(out_shapes),
        in_specs=[pl.BlockSpec(memory_space=pltpu.VMEM)] * len(operands),
        out_specs=tuple(pl.BlockSpec(memory_space=pltpu.VMEM) for _ in out_shapes),
        scratch_shapes=list(scratch),
        compiler_params=pltpu.CompilerParams(vmem_limit_bytes=vmem * MIB),
        cost_estimate=pl.CostEstimate(flops=flops, bytes_accessed=nbytes, transcendentals=0),
    )(*operands)


def shape(dims, dtype):
    return jax.ShapeDtypeStruct(dims, dtype)


def row_shift(block, down):
    rows = block.shape[0]
    place = lax.broadcasted_iota(jnp.int32, block.shape, 0) % 128
    if down:
        return jnp.where(place == 0, 0.0, pltpu.roll(block, 1, 0))
    return jnp.where(place == 127, 0.0, pltpu.roll(block, rows - 1, 0))


def three_shifts(haloed):
    wide = haloed.astype(F32)
    return (row_shift(wide, False).astype(BF16), haloed, row_shift(wide, True).astype(BF16))


def layer_call(kernel, outs, operands, weight, scratch, vmem, flops):
    vmem_spec = pl.BlockSpec(memory_space=pltpu.VMEM)
    return pl.pallas_call(
        kernel,
        out_shape=tuple(outs),
        in_specs=[vmem_spec] * (len(operands) + 1),
        out_specs=(vmem_spec,) * len(outs),
        scratch_shapes=scratch,
        compiler_params=pltpu.CompilerParams(vmem_limit_bytes=vmem * MIB),
        cost_estimate=pl.CostEstimate(flops=flops, bytes_accessed=5 * MIB, transcendentals=0),
    )(*operands, weight)


def pack_kernel(own, r1, r2, r3, grad, outer, *rest):
    *payload, turned = rest
    y = lax.axis_index("chan")
    space = lax.axis_index("space")
    first, z = space % 2 == 0, space // 8
    mine, far = grad[...], outer[...]
    three = jnp.where(
        first, jnp.concatenate([far, mine], axis=0), jnp.concatenate([mine, far], axis=0)
    )
    for step, part in enumerate((own, r1, r2, r3)):
        turn(part[...], turned.at[y ^ step])
    for step, out in enumerate(payload):
        out[:256, :] = turned[z ^ step]
        out[256:, :] = three


def pack(own, others, grad, outer):
    return call(
        pack_kernel,
        [shape((640, 256), BF16)] * 4,
        (own, *others, grad, outer),
        [pltpu.VMEM((4, 256, 256), BF16)],
        flops=10**9,
        vmem=8,
    )


def conv_kernel(own, r1, r2, r3, *rest):
    y = lax.axis_index("chan")
    first = lax.axis_index("space") % 2 == 0
    if len(rest) == 5:
        weight, core_out, inner_out, outer_out, field = rest
    else:
        three, weight, core_out, inner_out, outer_out, payload, field, turned = rest
        for step, part in enumerate((own, r1, r2, r3)):
            turn(part[...], turned.at[y ^ step])
        for z in range(4):
            payload[z, :256, :] = turned[z]
            payload[z, 256:, :] = three[...]
    for step, part in enumerate((own, r1, r2, r3)):
        for b in range(2):
            at = pl.multiple_of(b * 512 + (y ^ step) * 128, 128)
            field[:, pl.ds(at, 128)] = part[:, b * 128 : b * 128 + 128]
    values = field[...]
    sums = None
    for k in range(3):
        part = []
        for i in range(3):
            rhs = jnp.concatenate(
                [jnp.concatenate(pair(weight, i, k, b), axis=1) for b in range(2)], axis=0
            )
            part.append(jnp.dot(values, rhs, preferred_element_type=F32))
        planes = jnp.concatenate(
            [
                part[2][:128],
                part[1][:128] + part[2][128:],
                part[0][:128] + part[1][128:],
                part[0][128:],
            ],
            axis=0,
        )
        if k != 1:
            planes = row_shift(planes, k == 0)
        sums = planes if sums is None else sums + planes
    core_out[...] = sums[128:384]
    low = sums[:128].astype(BF16)
    high = sums[384:].astype(BF16)
    inner_out[...] = jnp.where(first, high, low)
    outer_out[...] = jnp.where(first, low, high)


def conv(own, others, weight, three=()):
    outs = [shape((256, 256), F32), shape((128, 256), BF16), shape((128, 256), BF16)]
    outs += [shape((4, 640, 256), BF16)] * len(three)
    scratch = [pltpu.VMEM((256, 1024), BF16)]
    scratch += [pltpu.VMEM((4, 256, 256), BF16)] * len(three)
    return layer_call(
        conv_kernel, outs, (own, *others, *three), weight, scratch, 16, 2 * 9 * 256 * 1024 * 256
    )


def conv_t_kernel(own, inner, outer, weight, *rest):
    *outs, three_out = rest
    y = lax.axis_index("chan")
    first = lax.axis_index("space") % 2 == 0
    low = jnp.where(first, outer[...], inner[...])
    high = jnp.where(first, inner[...], outer[...])
    haloed = jnp.concatenate([low, own[...], high], axis=0)
    three_out[...] = jnp.where(first, haloed[:384], haloed[128:])
    moved = three_shifts(haloed)
    lhs = jnp.concatenate([moved[k][(2 - i) * 128 : (2 - i) * 128 + 256] for i, k in TAPS], axis=1)
    for step in range(4):
        group = step if len(outs) == 1 else y ^ step
        out = outs[0].at[step] if len(outs) == 1 else outs[step]
        rows = pl.ds(group * 128 if len(outs) == 1 else pl.multiple_of(group * 128, 128), 128)
        rhs = jnp.concatenate(
            [
                jnp.concatenate(sum([pair(weight, i, k, b, rows) for i, k in TAPS], []), axis=1)
                for b in range(2)
            ],
            axis=0,
        )
        out[...] = lax.dot_general(
            lhs, rhs, (((1,), (1,)), ((), ())), preferred_element_type=F32
        ).astype(out.dtype)


def conv_t(own, inner, outer, weight, whole):
    if whole:
        outs = [shape((4, 256, 256), BF16)]
    else:
        outs = [shape((256, 256), F32)] + [shape((256, 256), BF16)] * 3
    outs += [shape((384, 256), BF16)]
    *parts, three = layer_call(
        conv_t_kernel, outs, (own, inner, outer), weight, [], 16, 2 * 9 * 256 * 256 * 1024
    )
    return parts, three


def turn(block, out):
    turned = block.T
    for half in range(2):
        for b in range(2):
            for x in range(4):
                source = b * 128 + x * 32 + half * 16
                target = half * 128 + b * 64 + x * 16
                out[target : target + 16, :] = turned[source : source + 16]


def middle_kernel(
    own, inner, outer, g0, g1, g2, g3, hidden_out, grad_out, inner_out, outer_out
):
    first = lax.axis_index("space") % 2 == 0
    zero = jnp.where(first, outer[...], inner[...]).astype(F32)
    one = jnp.where(first, inner[...], outer[...]).astype(F32)
    pre = own[...] + jnp.concatenate([zero, one], axis=0)
    hidden_grad = g0[...] + g1[...].astype(F32) + g2[...].astype(F32) + g3[...].astype(F32)
    sig = jax.nn.sigmoid(pre)
    hidden_out[...] = (pre * sig).astype(BF16)
    grad = (hidden_grad * sig * (1.0 + pre * (1.0 - sig))).astype(BF16)
    grad_out[...] = grad
    inner_out[...] = jnp.where(first, grad[128:], grad[:128])
    outer_out[...] = jnp.where(first, grad[:128], grad[128:])


def middle(own, inner, outer, parts):
    outs = [shape((256, 256), BF16)] * 2 + [shape((128, 256), BF16)] * 2
    return call(middle_kernel, outs, (own, inner, outer, *parts), flops=256 * 256 * 20, vmem=8)


def keep_product(total, tap, product):
    total[tap, :, 0:128] = product[64:, :128]
    total[tap, :, 128:256] = product[64:, 128:] + product[:64, :128]
    total[tap, :, 256:384] = product[:64, 128:]


def wprod_kernel(early, early_far, late, late_far, o0, o1, o2, o3, sums, total):
    space = lax.axis_index("space")
    core, z = space % 2, space // 8
    first = core == 0
    rows = pl.ds(pl.multiple_of(core * 128, 128), 128)

    def in_order(near, far, axis):
        return jnp.concatenate(
            [jnp.where(first, near, far), jnp.where(first, far, near)], axis=axis
        )

    for step in range(4):
        soon, soon_far = early.at[z ^ step], early_far.at[z ^ step]
        last, last_far = late.at[step], late_far.at[step]
        for layer in range(2):
            v, v_far, d, d_far = (
                (soon, soon_far, last, last_far) if layer == 0 else (last, last_far, soon, soon_far)
            )
            lhs = in_order(v[rows, :], v_far[rows, :], 1)
            moved = three_shifts(in_order(d[256:640, :], d_far[256:640, :], 0))
            for i, k in TAPS:
                at = (2 - i) * 128
                tap = 9 * layer + 3 * i + k
                product = jnp.dot(lhs, moved[k][at : at + 512], preferred_element_type=F32)
                if step == 0:
                    sums[tap] = product
                else:
                    sums[tap] += product
    for tap in range(18):
        total[tap, :, 0:128] = sums[tap, 64:, :128]
        total[tap, :, 128:256] = sums[tap, 64:, 128:] + sums[tap, :64, :128]
        total[tap, :, 256:384] = sums[tap, :64, 128:]
    x = (space // 2) % 4
    for step, out in enumerate((o0, o1, o2, o3)):
        chosen = pl.ds(pl.multiple_of((x ^ step) * 16, 16), 16)
        out[...] = total[:, chosen, :].astype(out.dtype)


def wprod(early, late):
    return call(
        wprod_kernel,
        [shape((18, 16, 384), F32)] + [shape((18, 16, 384), BF16)] * 3,
        (*early, *late),
        [pltpu.VMEM((18, 128, 256), F32), pltpu.VMEM((18, 64, 384), F32)],
        flops=4 * 9 * 128 * 2048 * 256,
    )


def last_kernel(own, r1, r2, r3, one_out, two_out):
    for layer, out in enumerate((one_out, two_out)):
        for i, k in TAPS:
            tap = 9 * layer + 3 * i + k
            total = own[tap] + r1[tap].astype(F32) + r2[tap].astype(F32) + r3[tap].astype(F32)
            for j in range(3):
                out[9 * i + 3 * j + k] = total[:, (2 - j) * 128 : (2 - j) * 128 + 128]


def last(parts):
    outs = call(last_kernel, [shape((27, 16, 128), F32)] * 2, parts, vmem=4)
    return [out.transpose(1, 0, 2) for out in outs]


def chip(z, x, core):
    return (z * 4 + x) * 2 + core


EVERY = [(z, x, core) for z in range(4) for x in range(4) for core in range(2)]


def over_chan(step):
    return [(i, i ^ step) for i in range(4)]


def over_z(step):
    return [(chip(z, x, c), chip(z ^ step, x, c)) for z, x, c in EVERY]


def over_x(step):
    return [(chip(z, x, c), chip(z, x ^ step, c)) for z, x, c in EVERY]


CORES = [(i, i ^ 1) for i in range(32)]
NEIGHBOURS = [(i, i + 1 if i % 2 else i - 1) for i in range(1, 31)]


def swap_halo(inner, outer):
    return lax.ppermute(inner, "space", CORES), lax.ppermute(outer, "space", NEIGHBOURS)


def cells_major(field):
    return field.transpose(1, 3, 2, 0).reshape(256, 256)


def channels_major(block):
    return block.reshape(2, 128, 2, 128).transpose(3, 0, 2, 1).astype(BF16)


def gather_chan(block):
    return [lax.ppermute(block, "chan", over_chan(step)) for step in (1, 2, 3)]


def scatter_chan(parts):
    return [parts[0]] + [
        lax.ppermute(parts[step], "chan", over_chan(step)) for step in (1, 2, 3)
    ]


def scatter_x(parts):
    return [parts[0]] + [lax.ppermute(parts[step], "space", over_x(step)) for step in (1, 2, 3)]


ALONG_Z = [[chip(z, x, c) for z in range(4)] for x in range(4) for c in range(2)]


def exchange_z(parts):
    return [parts[0]] + [lax.ppermute(parts[step], "space", over_z(step)) for step in (1, 2, 3)]


def with_far(near):
    return [near, lax.ppermute(near, "space", CORES)]


def add_halo(own, inner, outer):
    first = lax.axis_index("space") % 2 == 0
    zero = jnp.where(first, outer, inner).astype(F32)
    one = jnp.where(first, inner, outer).astype(F32)
    return own + jnp.concatenate([zero, one], axis=0)


def body(inputs, weight_one, weight_two, cotangent):
    core = lax.axis_index("space") % 2
    c_own = cells_major(cotangent)
    x_own = cells_major(inputs)
    w_two = weight_two.transpose(1, 0, 2)
    w_one = weight_one.transpose(1, 0, 2)
    c_inner, c_outer = swap_halo(
        lax.dynamic_slice_in_dim(c_own, (1 - core) * 128, 128, 0),
        lax.dynamic_slice_in_dim(c_own, core * 128, 128, 0),
    )
    x_others = gather_chan(x_own)
    hidden_parts, c_three = conv_t(c_own, c_inner, c_outer, w_two, False)
    hidden_parts = scatter_chan(hidden_parts)
    pre, low, high, payload = conv(x_own, x_others, w_one, [c_three])
    low, high = swap_halo(low, high)
    payload, hidden_parts, low = lax.optimization_barrier((payload, hidden_parts, low))
    early = lax.all_to_all(payload, "space", 0, 0, tiled=True, axis_index_groups=ALONG_Z)
    hidden, grad, g_inner, g_outer = middle(pre, low, high, hidden_parts)

    h_others = gather_chan(hidden)
    g_inner, g_outer = swap_halo(g_inner, g_outer)
    h_others, g_inner, early = lax.optimization_barrier((h_others, g_inner, early))
    early = with_far(early)
    payload = pack(hidden, h_others, grad, g_outer)
    payload, grad, hidden = lax.optimization_barrier((payload, grad, hidden))
    late = exchange_z(payload)
    input_parts, _ = conv_t(grad, g_inner, g_outer, w_one, False)
    input_parts = scatter_chan(input_parts)
    result, low, high = conv(hidden, h_others, w_two)
    late, input_parts, low = lax.optimization_barrier((late, input_parts, low))
    late = with_far(jnp.stack(late))
    shares = wprod(early, late)
    shares = scatter_x(shares)
    shares[1], low, high = lax.optimization_barrier((shares[1], low, high))
    grad_one, grad_two = last(shares)
    low, high = swap_halo(low, high)
    input_grad = sum(part.astype(F32) for part in input_parts)
    return (
        channels_major(add_halo(result, low, high)),
        channels_major(input_grad),
        grad_one,
        grad_two,
    )


def solution(mesh):
    placed = (
        P("chan", "space", None, None),
        P(None, None, "chan"),
        P(None, None, "chan"),
        P("chan", "space", None, None),
    )
    return jax.shard_map(
        body,
        mesh=mesh,
        in_specs=placed,
        out_specs=(
            P("chan", "space", None, None),
            P("chan", "space", None, None),
            P("space", None, "chan"),
            P("space", None, "chan"),
        ),
        check_vma=False,
    )
```

```python
import functools

import jax
import jax.numpy as jnp
from jax import lax
from jax.experimental import pallas as pl
from jax.experimental.pallas import tpu as pltpu
from jax.sharding import PartitionSpec as P

BF16 = jnp.bfloat16
F32 = jnp.float32
MIB = 1024 * 1024
TAPS = [(i, k) for i in range(3) for k in range(3)]
MET = ((1, 0), (2, 1))


def pair(weight, i, k, b, rows=slice(None)):
    return [weight[9 * i + 3 * j + k, rows, :] for j in MET[b]]


def call(kernel, out_shapes, operands, scratch=(), flops=0, vmem=16):
    nbytes = sum(a.size * a.dtype.itemsize for a in operands)
    nbytes += sum(a.size * a.dtype.itemsize for a in out_shapes)
    return pl.pallas_call(
        kernel,
        out_shape=tuple(out_shapes),
        in_specs=[pl.BlockSpec(memory_space=pltpu.VMEM)] * len(operands),
        out_specs=tuple(pl.BlockSpec(memory_space=pltpu.VMEM) for _ in out_shapes),
        scratch_shapes=list(scratch),
        compiler_params=pltpu.CompilerParams(vmem_limit_bytes=vmem * MIB),
        cost_estimate=pl.CostEstimate(flops=flops, bytes_accessed=nbytes, transcendentals=0),
    )(*operands)


def shape(dims, dtype):
    return jax.ShapeDtypeStruct(dims, dtype)


def row_shift(block, down):
    rows = block.shape[0]
    place = lax.broadcasted_iota(jnp.int32, block.shape, 0) % 128
    if down:
        return jnp.where(place == 0, 0.0, pltpu.roll(block, 1, 0))
    return jnp.where(place == 127, 0.0, pltpu.roll(block, rows - 1, 0))


def three_shifts(haloed):
    wide = haloed.astype(F32)
    return (row_shift(wide, False).astype(BF16), haloed, row_shift(wide, True).astype(BF16))


def layer_call(kernel, outs, operands, weight, scratch, vmem, flops):
    vmem_spec = pl.BlockSpec(memory_space=pltpu.VMEM)
    return pl.pallas_call(
        kernel,
        out_shape=tuple(outs),
        in_specs=[vmem_spec] * (len(operands) + 1),
        out_specs=(vmem_spec,) * len(outs),
        scratch_shapes=scratch,
        compiler_params=pltpu.CompilerParams(vmem_limit_bytes=vmem * MIB),
        cost_estimate=pl.CostEstimate(flops=flops, bytes_accessed=5 * MIB, transcendentals=0),
    )(*operands, weight)


def pack_kernel(own, r1, r2, r3, grad, outer, *rest):
    *payload, turned = rest
    y = lax.axis_index("chan")
    space = lax.axis_index("space")
    first, z = space % 2 == 0, space // 8
    mine, far = grad[...], outer[...]
    three = jnp.where(
        first, jnp.concatenate([far, mine], axis=0), jnp.concatenate([mine, far], axis=0)
    )
    for step, part in enumerate((own, r1, r2, r3)):
        turn(part[...], turned.at[y ^ step])
    for step, out in enumerate(payload):
        out[:256, :] = turned[z ^ step]
        out[256:, :] = three


def pack(own, others, grad, outer):
    return call(
        pack_kernel,
        [shape((640, 256), BF16)] * 4,
        (own, *others, grad, outer),
        [pltpu.VMEM((4, 256, 256), BF16)],
        flops=10**9,
        vmem=8,
    )


def conv_kernel(own, r1, r2, r3, *rest):
    y = lax.axis_index("chan")
    first = lax.axis_index("space") % 2 == 0
    if len(rest) == 5:
        weight, core_out, inner_out, outer_out, field = rest
    else:
        three, weight, core_out, inner_out, outer_out, payload, field, turned = rest
        for step, part in enumerate((own, r1, r2, r3)):
            turn(part[...], turned.at[y ^ step])
        for z in range(4):
            payload[z, :256, :] = turned[z]
            payload[z, 256:, :] = three[...]
    for step, part in enumerate((own, r1, r2, r3)):
        for b in range(2):
            at = pl.multiple_of(b * 512 + (y ^ step) * 128, 128)
            field[:, pl.ds(at, 128)] = part[:, b * 128 : b * 128 + 128]
    values = field[...]
    sums = None
    for k in range(3):
        part = []
        for i in range(3):
            rhs = jnp.concatenate(
                [jnp.concatenate(pair(weight, i, k, b), axis=1) for b in range(2)], axis=0
            )
            part.append(jnp.dot(values, rhs, preferred_element_type=F32))
        planes = jnp.concatenate(
            [
                part[2][:128],
                part[1][:128] + part[2][128:],
                part[0][:128] + part[1][128:],
                part[0][128:],
            ],
            axis=0,
        )
        if k != 1:
            planes = row_shift(planes, k == 0)
        sums = planes if sums is None else sums + planes
    core_out[...] = sums[128:384]
    low = sums[:128].astype(BF16)
    high = sums[384:].astype(BF16)
    inner_out[...] = jnp.where(first, high, low)
    outer_out[...] = jnp.where(first, low, high)


def conv(own, others, weight, three=()):
    outs = [shape((256, 256), F32), shape((128, 256), BF16), shape((128, 256), BF16)]
    outs += [shape((4, 640, 256), BF16)] * len(three)
    scratch = [pltpu.VMEM((256, 1024), BF16)]
    scratch += [pltpu.VMEM((4, 256, 256), BF16)] * len(three)
    return layer_call(
        conv_kernel, outs, (own, *others, *three), weight, scratch, 16, 2 * 9 * 256 * 1024 * 256
    )


def conv_t_kernel(own, inner, outer, weight, *rest):
    *outs, three_out = rest
    y = lax.axis_index("chan")
    first = lax.axis_index("space") % 2 == 0
    low = jnp.where(first, outer[...], inner[...])
    high = jnp.where(first, inner[...], outer[...])
    haloed = jnp.concatenate([low, own[...], high], axis=0)
    three_out[...] = jnp.where(first, haloed[:384], haloed[128:])
    moved = three_shifts(haloed)
    lhs = jnp.concatenate([moved[k][(2 - i) * 128 : (2 - i) * 128 + 256] for i, k in TAPS], axis=1)
    for step in range(4):
        group = step if len(outs) == 1 else y ^ step
        out = outs[0].at[step] if len(outs) == 1 else outs[step]
        rows = pl.ds(group * 128 if len(outs) == 1 else pl.multiple_of(group * 128, 128), 128)
        rhs = jnp.concatenate(
            [
                jnp.concatenate(sum([pair(weight, i, k, b, rows) for i, k in TAPS], []), axis=1)
                for b in range(2)
            ],
            axis=0,
        )
        out[...] = lax.dot_general(
            lhs, rhs, (((1,), (1,)), ((), ())), preferred_element_type=F32
        ).astype(out.dtype)


def conv_t(own, inner, outer, weight, whole):
    if whole:
        outs = [shape((4, 256, 256), BF16)]
    else:
        outs = [shape((256, 256), F32)] + [shape((256, 256), BF16)] * 3
    outs += [shape((384, 256), BF16)]
    *parts, three = layer_call(
        conv_t_kernel, outs, (own, inner, outer), weight, [], 16, 2 * 9 * 256 * 256 * 1024
    )
    return parts, three


def turn(block, out):
    turned = block.T
    for half in range(2):
        for b in range(2):
            for x in range(4):
                source = b * 128 + x * 32 + half * 16
                target = half * 128 + b * 64 + x * 16
                out[target : target + 16, :] = turned[source : source + 16]


def middle_kernel(
    own, inner, outer, g0, g1, g2, g3, hidden_out, grad_out, inner_out, outer_out
):
    first = lax.axis_index("space") % 2 == 0
    zero = jnp.where(first, outer[...], inner[...]).astype(F32)
    one = jnp.where(first, inner[...], outer[...]).astype(F32)
    pre = own[...] + jnp.concatenate([zero, one], axis=0)
    hidden_grad = g0[...] + g1[...].astype(F32) + g2[...].astype(F32) + g3[...].astype(F32)
    sig = jax.nn.sigmoid(pre)
    hidden_out[...] = (pre * sig).astype(BF16)
    grad = (hidden_grad * sig * (1.0 + pre * (1.0 - sig))).astype(BF16)
    grad_out[...] = grad
    inner_out[...] = jnp.where(first, grad[128:], grad[:128])
    outer_out[...] = jnp.where(first, grad[:128], grad[128:])


def middle(own, inner, outer, parts):
    outs = [shape((256, 256), BF16)] * 2 + [shape((128, 256), BF16)] * 2
    return call(middle_kernel, outs, (own, inner, outer, *parts), flops=256 * 256 * 20, vmem=8)


def keep_product(total, tap, product):
    total[tap, :, 0:128] = product[64:, :128]
    total[tap, :, 128:256] = product[64:, 128:] + product[:64, :128]
    total[tap, :, 256:384] = product[:64, 128:]


def wprod_kernel(early, early_far, late, late_far, o0, o1, o2, o3, sums, total):
    space = lax.axis_index("space")
    core, z = space % 2, space // 8
    first = core == 0
    rows = pl.ds(pl.multiple_of(core * 128, 128), 128)

    def in_order(near, far, axis):
        return jnp.concatenate(
            [jnp.where(first, near, far), jnp.where(first, far, near)], axis=axis
        )

    for step in range(4):
        soon, soon_far = early.at[z ^ step], early_far.at[z ^ step]
        last, last_far = late.at[step], late_far.at[step]
        for layer in range(2):
            v, v_far, d, d_far = (
                (soon, soon_far, last, last_far) if layer == 0 else (last, last_far, soon, soon_far)
            )
            lhs = in_order(v[rows, :], v_far[rows, :], 1)
            moved = three_shifts(in_order(d[256:640, :], d_far[256:640, :], 0))
            for i, k in TAPS:
                at = (2 - i) * 128
                tap = 9 * layer + 3 * i + k
                product = jnp.dot(lhs, moved[k][at : at + 512], preferred_element_type=F32)
                if step == 0:
                    sums[tap] = product
                else:
                    sums[tap] += product
    for tap in range(18):
        total[tap, :, 0:128] = sums[tap, 64:, :128]
        total[tap, :, 128:256] = sums[tap, 64:, 128:] + sums[tap, :64, :128]
        total[tap, :, 256:384] = sums[tap, :64, 128:]
    x = (space // 2) % 4
    for step, out in enumerate((o0, o1, o2, o3)):
        chosen = pl.ds(pl.multiple_of((x ^ step) * 16, 16), 16)
        out[...] = total[:, chosen, :].astype(out.dtype)


def wprod(early, late):
    return call(
        wprod_kernel,
        [shape((18, 16, 384), F32)] + [shape((18, 16, 384), BF16)] * 3,
        (*early, *late),
        [pltpu.VMEM((18, 128, 256), F32), pltpu.VMEM((18, 64, 384), F32)],
        flops=4 * 9 * 128 * 2048 * 256,
    )


def last_kernel(own, r1, r2, r3, one_out, two_out):
    for layer, out in enumerate((one_out, two_out)):
        for i, k in TAPS:
            tap = 9 * layer + 3 * i + k
            total = own[tap] + r1[tap].astype(F32) + r2[tap].astype(F32) + r3[tap].astype(F32)
            for j in range(3):
                out[9 * i + 3 * j + k] = total[:, (2 - j) * 128 : (2 - j) * 128 + 128]


def last(parts):
    outs = call(last_kernel, [shape((27, 16, 128), F32)] * 2, parts, vmem=4)
    return [out.transpose(1, 0, 2) for out in outs]


def chip(z, x, core):
    return (z * 4 + x) * 2 + core


EVERY = [(z, x, core) for z in range(4) for x in range(4) for core in range(2)]


def over_chan(step):
    return [(i, i ^ step) for i in range(4)]


def over_z(step):
    return [(chip(z, x, c), chip(z ^ step, x, c)) for z, x, c in EVERY]


def over_x(step):
    return [(chip(z, x, c), chip(z, x ^ step, c)) for z, x, c in EVERY]


CORES = [(i, i ^ 1) for i in range(32)]
NEIGHBOURS = [(i, i + 1 if i % 2 else i - 1) for i in range(1, 31)]


def swap_halo(inner, outer):
    return lax.ppermute(inner, "space", CORES), lax.ppermute(outer, "space", NEIGHBOURS)


def cells_major(field):
    return field.transpose(1, 3, 2, 0).reshape(256, 256)


def channels_major(block):
    return block.reshape(2, 128, 2, 128).transpose(3, 0, 2, 1).astype(BF16)


def gather_chan(block):
    return [lax.ppermute(block, "chan", over_chan(step)) for step in (1, 2, 3)]


def scatter_chan(parts):
    return [parts[0]] + [
        lax.ppermute(parts[step], "chan", over_chan(step)) for step in (1, 2, 3)
    ]


def scatter_x(parts):
    return [parts[0]] + [lax.ppermute(parts[step], "space", over_x(step)) for step in (1, 2, 3)]


ALONG_Z = [[chip(z, x, c) for z in range(4)] for x in range(4) for c in range(2)]


def exchange_z(parts):
    return [parts[0]] + [lax.ppermute(parts[step], "space", over_z(step)) for step in (1, 2, 3)]


def with_far(near):
    return [near, lax.ppermute(near, "space", CORES)]


def add_halo(own, inner, outer):
    first = lax.axis_index("space") % 2 == 0
    zero = jnp.where(first, outer, inner).astype(F32)
    one = jnp.where(first, inner, outer).astype(F32)
    return own + jnp.concatenate([zero, one], axis=0)


def body(inputs, weight_one, weight_two, cotangent):
    core = lax.axis_index("space") % 2
    c_own = cells_major(cotangent)
    x_own = cells_major(inputs)
    w_two = weight_two.transpose(1, 0, 2)
    w_one = weight_one.transpose(1, 0, 2)
    c_inner, c_outer = swap_halo(
        lax.dynamic_slice_in_dim(c_own, (1 - core) * 128, 128, 0),
        lax.dynamic_slice_in_dim(c_own, core * 128, 128, 0),
    )
    x_others = gather_chan(x_own)
    hidden_parts, c_three = conv_t(c_own, c_inner, c_outer, w_two, False)
    hidden_parts = scatter_chan(hidden_parts)
    pre, low, high, payload = conv(x_own, x_others, w_one, [c_three])
    low, high = swap_halo(low, high)
    payload, hidden_parts, low, high = lax.optimization_barrier(
        (payload, hidden_parts, low, high)
    )
    early = lax.all_to_all(payload, "space", 0, 0, tiled=True, axis_index_groups=ALONG_Z)
    hidden, grad, g_inner, g_outer = middle(pre, low, high, hidden_parts)

    h_others = gather_chan(hidden)
    g_inner, g_outer = swap_halo(g_inner, g_outer)
    payload = pack(hidden, h_others, grad, g_outer)
    payload, grad, hidden = lax.optimization_barrier((payload, grad, hidden))
    late = exchange_z(payload)
    input_parts, _ = conv_t(grad, g_inner, g_outer, w_one, False)
    input_parts = scatter_chan(input_parts)
    result, low, high = conv(hidden, h_others, w_two)
    late, input_parts, low, early = lax.optimization_barrier((late, input_parts, low, early))
    early = with_far(early)
    late = with_far(jnp.stack(late))
    shares = wprod(early, late)
    shares = scatter_x(shares)
    shares[1], low, high = lax.optimization_barrier((shares[1], low, high))
    grad_one, grad_two = last(shares)
    low, high = swap_halo(low, high)
    input_grad = sum(part.astype(F32) for part in input_parts)
    return (
        channels_major(add_halo(result, low, high)),
        channels_major(input_grad),
        grad_one,
        grad_two,
    )


def solution(mesh):
    placed = (
        P("chan", "space", None, None),
        P(None, None, "chan"),
        P(None, None, "chan"),
        P("chan", "space", None, None),
    )
    return jax.shard_map(
        body,
        mesh=mesh,
        in_specs=placed,
        out_specs=(
            P("chan", "space", None, None),
            P("chan", "space", None, None),
            P("space", None, "chan"),
            P("space", None, "chan"),
        ),
        check_vma=False,
    )
```
